32 devices in a mesh: dp: 8 (over y, x, core), mp: 4 (over z).
Axes of the slice: x: 2, y: 2, z: 4, core: 2. Of those that a mesh axis runs over, the one named last changes fastest.
Arguments:
- act_in: bfloat16 [1024, 4096], P('dp', 'mp'), may hold values from -6 to 6
- grad_in: bfloat16 [1024, 16384], P('dp'), may hold values from -6 to 6
- query_act: bfloat16 [1024, 4096], P('dp', 'mp'), may hold values from -6 to 6
- query_grad: bfloat16 [1024, 16384], P('dp'), may hold values from -6 to 6
- act_basis: bfloat16 [4096, 128], P('mp'), may hold values from -1.1 to 1.1
- grad_basis: bfloat16 [16384, 128], P('dp'), may hold values from -1.1 to 1.1
- seq_lengths: int32 [4], replicated, may hold values from 1 to 256, 768 in all
Outputs:
- moments: float32 [4096, 16384], P('mp', 'dp')
- scores: float32 [64, 4], replicated
The draws below stay inside these ranges and needn't reach their ends.
Inputs may be any that keep to these rules, and one draw needn't show every extreme that they name: `seq_lengths`: live tokens are the first ones of each sequence, and one sequence is full.
All inputs are finite; a program needn't handle non-finite values.
Results may differ from the reference program's by a relative error of at most 0.0046.
Values may be sent and summed in bfloat16 or wider, within the bound.
A program may use at most 192 MiB of HBM per device.

```python
import math
import jax
import jax.numpy as jnp
import numpy as np
from jax import lax

D = 4096
FF = 16384
BLOCK = 128
SEQS = 4
QUERIES = 64
QUERY_LEN = 16
TOKENS = 1024
SEQ_LEN = 256
QROWS = 1024


def basis_blocks(key, total_rows):
    first_key, second_key = jax.random.split(key)
    base = jnp.clip(jax.random.normal(first_key, (total_rows, BLOCK), jnp.float32), -4.0, 4.0)
    column_scale = jnp.exp(jax.random.uniform(second_key, (total_rows // BLOCK, 1, BLOCK), jnp.float32, math.log(0.3), math.log(3.0)))
    blocks = base.reshape(total_rows // BLOCK, BLOCK, BLOCK) * column_scale / math.sqrt(BLOCK)
    blocks = jnp.clip(blocks, -1.09375, 1.09375)
    return blocks.reshape(total_rows, BLOCK).astype(jnp.bfloat16)


def draw_act_basis(key, part):
    return basis_blocks(jax.random.fold_in(key, 11), D)


def draw_grad_basis(key, part):
    return basis_blocks(jax.random.fold_in(key, 23), FF)


def level_of(key, shape, cuts, smallest, top_value):
    factor_of = 1.0
    for dim, blocks in cuts:
        steps = jax.random.uniform(jax.random.fold_in(jax.random.fold_in(key, 6), dim), (blocks,), jnp.float32, smallest / len(cuts), top_value / len(cuts))
        factor_of = factor_of * jnp.repeat(jnp.exp(steps), shape[dim] // blocks).reshape((-1,) + (1,) * (len(shape) - 1 - dim))
    return factor_of


def split_up(number_of, total, limit, skew):
    portions = [(1 << 20) // math.isqrt(rank ** skew) + 1 for rank in range(2, number_of + 1)]
    spare, given = total - limit - (number_of - 1), [1] * (number_of - 1)
    while spare > 0:
        movable = [i for i in range(number_of - 1) if given[i] < limit]
        whole, remaining = sum([portions[i] for i in movable]), spare
        for i in movable:
            more = min(limit - given[i], max(1, remaining * portions[i] // whole), spare)
            given[i] = given[i] + more
            spare = spare - more
    return np.array([limit] + given)


def uneven(stream_key, amount, total, reach, slope):
    if amount == 2:
        one = jax.random.randint(stream_key, (), max(1, total - reach), min(reach, total - 1) + 1)
        return jnp.stack([one, total - one])
    sizes = jnp.asarray(split_up(amount, total, reach, slope), jnp.int32)
    pairs = (amount - 1) // 2
    donor, sink = sizes[1:1 + 2 * pairs:2], sizes[2:2 + 2 * pairs:2]
    margin = jnp.minimum(donor - 1, reach - sink)
    shifted = jax.random.randint(jax.random.fold_in(stream_key, 1), (pairs,), 0, 1 << 20) % (margin + 1)
    sizes = sizes.at[1:1 + 2 * pairs:2].set(donor - shifted).at[2:2 + 2 * pairs:2].set(sink + shifted)
    return sizes[jax.random.permutation(jax.random.fold_in(stream_key, 2), amount)]


def bell_draw(own_key, shape, width, limit, cuts=(), kind=jnp.bfloat16):
    entries = width * jax.random.normal(own_key, shape, jnp.float32)
    if cuts:
        entries = entries * level_of(own_key, shape, cuts, -0.22, 0.18)
    return jnp.clip(entries, -limit, limit).astype(kind)


def setup_inputs(seed: int = 0) -> dict:
    seeds = jax.random.split(jax.random.key(seed), 8)
    return {
        "act_in": bell_draw(seeds[0], (TOKENS, D), 1.0, 6.0, ((0, 8), (1, 4))),
        "grad_in": bell_draw(seeds[1], (TOKENS, FF), 1.0, 6.0, ((0, 8),)),
        "query_act": bell_draw(seeds[2], (QROWS, D), 1.0, 6.0, ((0, 8), (1, 4))),
        "query_grad": bell_draw(seeds[3], (QROWS, FF), 1.0, 6.0, ((0, 8),)),
        "act_basis": draw_act_basis(jax.random.fold_in(seeds[7], 71), 0),
        "grad_basis": draw_grad_basis(jax.random.fold_in(seeds[7], 71), 0),
        "seq_lengths": uneven(seeds[6], SEQS, SEQS * SEQ_LEN * 3 // 4, SEQ_LEN, 0).astype(jnp.int32),
    }


damping = 0.1

def rotate(rows_in, basis_rows):
    count_rows, full_width = rows_in.shape
    block_size = basis_rows.shape[1]
    blocks = full_width // block_size
    product = jnp.einsum('nbk,bkc->nbc', rows_in.reshape(count_rows, blocks, block_size).astype(jnp.float32), basis_rows.reshape(blocks, block_size, block_size).astype(jnp.float32))
    return product.reshape(count_rows, full_width)

def reference(act_in, grad_in, query_act, query_grad, act_basis, grad_basis, seq_lengths):
    position = jnp.arange(TOKENS, dtype=jnp.int32)
    seq_index = (position // SEQ_LEN).astype(jnp.int32)
    within = position % SEQ_LEN
    live_rows = (within < seq_lengths[seq_index]).astype(jnp.float32)
    act_rot = (rotate(act_in, act_basis) * live_rows[:, None]).astype(jnp.bfloat16)
    grad_rot = rotate(grad_in, grad_basis).astype(jnp.bfloat16)
    query_act_rot = rotate(query_act, act_basis).astype(jnp.bfloat16)
    query_grad_rot = rotate(query_grad, grad_basis).astype(jnp.bfloat16)
    act_square = jnp.square(act_rot.astype(jnp.float32)).astype(jnp.bfloat16)
    grad_square = jnp.square(grad_rot.astype(jnp.float32)).astype(jnp.bfloat16)
    counted = jnp.sum(seq_lengths).astype(jnp.float32)
    moments = jnp.dot(act_square.T, grad_square, preferred_element_type=jnp.float32) / counted
    weights = 1.0 / (moments + damping)
    scale_seq = lax.rsqrt(seq_lengths.astype(jnp.float32))

    def one_sequence(inputs):
        seq_acts, seq_grads, scale_one = inputs
        seq_grad = jnp.dot(seq_acts.T, seq_grads, preferred_element_type=jnp.float32)
        precond = (weights * seq_grad * scale_one).astype(jnp.bfloat16)
        mapped = jnp.dot(query_act_rot, precond, preferred_element_type=jnp.float32)
        per_row = lax.optimization_barrier(jnp.sum(mapped * query_grad_rot.astype(jnp.float32), axis=1))
        return lax.optimization_barrier(jnp.sum(per_row.reshape(QUERIES, QUERY_LEN), axis=1))
    columns = lax.map(one_sequence, (act_rot.reshape(SEQS, SEQ_LEN, D), grad_rot.reshape(SEQS, SEQ_LEN, FF), scale_seq))
    scores = columns.T / math.sqrt(QUERY_LEN * D * FF)
    return (moments, scores)
```

```python
import functools
import math

import jax
import jax.numpy as jnp
from jax import lax
from jax.experimental import pallas as pl
from jax.experimental.pallas import tpu as pltpu
from jax.sharding import PartitionSpec as P

D = 4096
FF = 16384
QUERIES = 64
QUERY_LEN = 16

damping = 0.1
MESH = pl.DeviceIdType.MESH


def flipped(index, mask):
    bit = 1
    while bit <= mask:
        if mask & bit:
            index = index + bit * (1 - 2 * ((index // bit) % 2))
        bit *= 2
    return index


def kernel(
    dp_count, mp_count, chunks, shared_train, shared_query,
    lengths, act_in, grad_in, query_act, query_grad, act_basis_in, grad_basis_in,
    moments, partial,
    act_raw, qact_raw, grad_raw, qgrad_raw, act_basis, grad_basis,
    act_t, q_rot, precond, staged, totals,
    act_send, act_recv, qact_send, qact_recv, grad_send, grad_recv, qgrad_send, qgrad_recv,
    pass_send, pass_recv, qpass_send, qpass_recv, local_sem, out_sem,
):
    me = lax.axis_index("dp")
    mine = lax.axis_index("mp")
    seq_count = lengths.shape[0]
    tok_dev, act_width = act_in.shape
    q_dev = query_act.shape[0]
    cols = grad_raw.shape[2]
    block = act_basis_in.shape[1]
    tiles, _, tile = staged.shape
    tokens = tok_dev * dp_count
    seq_len = tokens // seq_count
    q_rows = q_dev * dp_count
    chunk_cols = cols // chunks
    masks = list(range(1, dp_count))
    peers = {k: flipped(me, k) for k in masks}

    barrier = pltpu.get_barrier_semaphore()
    for k in masks:
        pl.semaphore_signal(barrier, inc=1, device_id={"dp": peers[k], "mp": mine}, device_id_type=MESH)
    others = [lax.rem(mine + step, mp_count) for step in range(1, mp_count)]
    for other in others:
        pl.semaphore_signal(barrier, inc=1, device_id={"dp": me, "mp": other}, device_id_type=MESH)

    locals_in = [
        pltpu.make_async_copy(act_in, act_raw.at[me], local_sem.at[0]),
        pltpu.make_async_copy(act_basis_in, act_basis, local_sem.at[1]),
        pltpu.make_async_copy(grad_basis_in, grad_basis, local_sem.at[2]),
        pltpu.make_async_copy(
            grad_in.at[:, pl.ds(pl.multiple_of(me * cols, 128), cols)], grad_raw.at[me], local_sem.at[3]),
        pltpu.make_async_copy(query_act, qact_raw.at[me], local_sem.at[4]),
        pltpu.make_async_copy(
            query_grad.at[:, pl.ds(pl.multiple_of(me * cols, 128), cols)], qgrad_raw.at[me], local_sem.at[5]),
    ]
    for copy in locals_in:
        copy.start()
    pl.semaphore_wait(barrier, len(masks) + len(others))

    def remote(src, dst, send, recv, dp, mp):
        return pltpu.make_async_remote_copy(
            src_ref=src, dst_ref=dst, send_sem=send, recv_sem=recv,
            device_id={"dp": dp, "mp": mp}, device_id_type=MESH)

    sends = []

    def begin(copy):
        copy.start()
        sends.append(copy)

    act_masks = [k for k in masks if k == 1 or k % 2 == 0]

    def send_acts(src, raw, send, recv):
        for k in reversed(act_masks):
            begin(remote(src, raw.at[me], send.at[k], recv.at[k], peers[k], mine))

    def part_of(owner, rows):
        return pl.ds(pl.multiple_of(owner * (rows // mp_count), 16), rows // mp_count)

    def send_shared(src, raw, send, recv, shared):
        rows = part_of(mine, src.shape[0])
        for k in reversed(shared):
            there = pl.ds(pl.multiple_of(peers[k] * cols, 128), cols)
            begin(remote(
                src.at[rows, there], raw.at[me, rows, :], send.at[0, k], recv.at[0, k], peers[k], mine))

    def send_grads(src, raw, send, recv, shared, start, width, slot):
        for k in reversed(masks):
            if k not in shared:
                there = pl.ds(pl.multiple_of(peers[k] * cols + start, 128), width)
                begin(remote(
                    src.at[:, there], raw.at[me, :, pl.ds(start, width)],
                    send.at[slot, k], recv.at[slot, k], peers[k], mine))

    send_acts(act_in, act_raw, act_send, act_recv)
    send_shared(grad_in, grad_raw, grad_send, grad_recv, shared_train)
    send_grads(grad_in, grad_raw, grad_send, grad_recv, shared_train, 0, cols, 0)
    send_acts(query_act, qact_raw, qact_send, qact_recv)
    send_shared(query_grad, qgrad_raw, qgrad_send, qgrad_recv, shared_query)
    for c in range(chunks):
        send_grads(query_grad, qgrad_raw, qgrad_send, qgrad_recv, shared_query, c * chunk_cols, chunk_cols, c)

    def arrived(ref, send, recv):
        remote(ref, ref, send, recv, peers[1], mine).wait_recv()

    def relay_acts(raw, send, recv):
        for k in reversed(act_masks):
            arrived(raw.at[peers[k]], send.at[k], recv.at[k])
            if k > 1:
                here = raw.at[peers[k]]
                begin(remote(here, here, send.at[k + 1], recv.at[k + 1], peers[1], mine))

    def finish_acts(raw, send, recv):
        for k in masks:
            if k not in act_masks:
                arrived(raw.at[peers[k]], send.at[k], recv.at[k])

    def relay_grads(raw, send, recv, fsend, frecv, shared):
        for n, k in enumerate(reversed(shared)):
            here = raw.at[peers[k], part_of(mine, raw.shape[1]), :]
            arrived(here, send.at[0, k], recv.at[0, k])
            for step, other in enumerate(others):
                begin(remote(here, here, fsend.at[n, step], frecv.at[n, step], me, other))

    def finish_grads(raw, send, recv, shared, start, width, slot):
        for k in reversed(masks):
            if k not in shared:
                arrived(raw.at[peers[k], :, pl.ds(start, width)], send.at[slot, k], recv.at[slot, k])

    def finish_shared(raw, fsend, frecv, shared):
        for n, k in enumerate(reversed(shared)):
            for step in range(mp_count - 1):
                owner = lax.rem(mine + (mp_count - 1 - step), mp_count)
                arrived(
                    raw.at[peers[k], part_of(owner, raw.shape[1]), :], fsend.at[n, step], frecv.at[n, step])

    relay_acts(act_raw, act_send, act_recv)
    finish_acts(act_raw, act_send, act_recv)
    relay_grads(grad_raw, grad_send, grad_recv, pass_send, pass_recv, shared_train)
    for copy in locals_in:
        copy.wait()

    limits = [lengths[s] for s in range(seq_count)]
    counted = limits[0]
    for s in range(1, seq_count):
        counted = counted + limits[s]
    inverse = 1.0 / jnp.full((1, tile), counted.astype(jnp.float32), jnp.float32)

    @pl.loop(0, dp_count)
    def _(e):
        where_tok = e * tok_dev + lax.broadcasted_iota(jnp.int32, (block, tok_dev), 1)
        live = jnp.zeros((block, tok_dev), jnp.float32)
        for s in range(seq_count):
            inside = (where_tok >= s * seq_len) & (where_tok < s * seq_len + limits[s])
            live = jnp.where(inside, 1.0, live)
        for b in range(act_width // block):
            span = pl.ds(b * block, block)
            turned = lax.dot_general(
                act_basis[span, :].T, act_raw[e, :, span], (((1,), (1,)), ((), ())),
                preferred_element_type=jnp.float32)
            act_t[span, pl.ds(pl.multiple_of(e * tok_dev, 128), tok_dev)] = (turned * live).astype(jnp.bfloat16)

    def wide_basis(jt):
        first = grad_basis[pl.ds(pl.multiple_of(jt * tile, 128), block), :]
        rows = []
        count = tile // block
        zero = jnp.zeros_like(first)
        for h in range(count):
            own = grad_basis[pl.ds(pl.multiple_of(jt * tile + h * block, 128), block), :]
            rows.append(jnp.concatenate([own if g == h else zero for g in range(count)], axis=1))
        return jnp.concatenate(rows, axis=0)

    def turned_grads(raw, jt, rows):
        span = pl.ds(pl.multiple_of(jt * tile, 128), tile)
        whole = raw[:, :, span].reshape(rows, tile)
        return jnp.dot(whole, wide_basis(jt), preferred_element_type=jnp.float32).astype(jnp.bfloat16)

    finish_shared(grad_raw, pass_send, pass_recv, shared_train)
    finish_grads(grad_raw, grad_send, grad_recv, shared_train, 0, cols, 0)

    def out_copy(jt):
        span = pl.ds(pl.multiple_of(jt * tile, 128), tile)
        return pltpu.make_async_copy(staged.at[jt], moments.at[:, span], out_sem.at[jt])

    per_chunk = tiles // chunks

    def first_phase(jt):
        grads = turned_grads(grad_raw, jt, tokens)
        total = jnp.zeros((act_width, tile), jnp.float32)
        for s in range(seq_count):
            a = act_t[:, s * seq_len:(s + 1) * seq_len]
            g = grads[s * seq_len:(s + 1) * seq_len, :]
            total = total + jnp.dot(a * a, g * g, preferred_element_type=jnp.float32)
        total = total * inverse
        staged[jt] = total
        weights = 1.0 / (total + damping)
        for s in range(seq_count):
            a = act_t[:, s * seq_len:(s + 1) * seq_len]
            g = grads[s * seq_len:(s + 1) * seq_len, :]
            precond[s, jt] = (weights * jnp.dot(a, g, preferred_element_type=jnp.float32)).astype(jnp.bfloat16)
        out_copy(jt).start()

    half = tiles // 2
    pl.loop(0, half)(first_phase)
    relay_acts(qact_raw, qact_send, qact_recv)
    relay_grads(qgrad_raw, qgrad_send, qgrad_recv, qpass_send, qpass_recv, shared_query)
    pl.loop(half, tiles)(first_phase)
    finish_acts(qact_raw, qact_send, qact_recv)

    @pl.loop(0, dp_count)
    def _(e):
        for b in range(act_width // block):
            span = pl.ds(b * block, block)
            turned = jnp.dot(qact_raw[e, :, span], act_basis[span, :], preferred_element_type=jnp.float32)
            q_rot[pl.ds(pl.multiple_of(e * q_dev, 16), q_dev), span] = turned.astype(jnp.bfloat16)

    totals[...] = jnp.zeros_like(totals)
    finish_shared(qgrad_raw, qpass_send, qpass_recv, shared_query)

    def second_phase(jt):
        grads = turned_grads(qgrad_raw, jt, q_rows).astype(jnp.float32)
        for s in range(seq_count):
            mapped = jnp.dot(q_rot[...], precond[s, jt], preferred_element_type=jnp.float32) * grads
            folded = mapped[:, :128]
            for h in range(1, tile // 128):
                folded = folded + mapped[:, h * 128:(h + 1) * 128]
            totals[s] += folded.reshape(QUERIES, q_rows // QUERIES // 8, 8, 128).sum(axis=1)

    for c in range(chunks):
        finish_grads(qgrad_raw, qgrad_send, qgrad_recv, shared_query, c * chunk_cols, chunk_cols, c)
        pl.loop(c * per_chunk, (c + 1) * per_chunk)(second_phase)

    lane = lax.broadcasted_iota(jnp.int32, (QUERIES, 128), 1)
    answer = jnp.zeros((QUERIES, 128), jnp.float32)
    for s in range(seq_count):
        row = jnp.sum(jnp.sum(totals[s], axis=1), axis=1, keepdims=True)
        answer = jnp.where(lane == s, row, answer)
    partial[...] = answer

    for jt in range(tiles):
        out_copy(jt).wait()
    for copy in sends:
        copy.wait_send()


def local(act_in, grad_in, query_act, query_grad, act_basis, grad_basis, seq_lengths):
    dp_count = lax.axis_size("dp")
    mp_count = lax.axis_size("mp")
    tok_dev, act_width = act_in.shape
    q_dev = query_act.shape[0]
    cols = grad_in.shape[1] // dp_count
    seq_count = seq_lengths.shape[0]
    tokens, q_rows = tok_dev * dp_count, q_dev * dp_count
    tile = min(256, cols)
    tiles = cols // tile
    chunks = min(4, tiles)
    far = [k for k in range(1, dp_count) if bin(k >> 1).count("1") >= 2]
    shared_train = far if tok_dev % (16 * mp_count) == 0 and dp_count <= 2 * tiles else []
    shared_query = far if q_dev % (16 * mp_count) == 0 and dp_count <= 2 * tiles else []
    steps = max(1, mp_count - 1)
    dma = pltpu.SemaphoreType.DMA
    any_space = pl.BlockSpec(memory_space=pl.ANY)
    bf16 = jnp.bfloat16
    moments, partial = pl.pallas_call(
        functools.partial(kernel, dp_count, mp_count, chunks, shared_train, shared_query),
        out_shape=(
            jax.ShapeDtypeStruct((act_width, cols), jnp.float32),
            jax.ShapeDtypeStruct((QUERIES, 128), jnp.float32),
        ),
        in_specs=[pl.BlockSpec(memory_space=pltpu.SMEM)] + [any_space] * 6,
        out_specs=(any_space, pl.BlockSpec(memory_space=pltpu.VMEM)),
        scratch_shapes=[
            pltpu.VMEM((dp_count, tok_dev, act_width), bf16),
            pltpu.VMEM((dp_count, q_dev, act_width), bf16),
            pltpu.VMEM((dp_count, tok_dev, cols), bf16),
            pltpu.VMEM((dp_count, q_dev, cols), bf16),
            pltpu.VMEM(act_basis.shape, bf16),
            pltpu.VMEM(grad_basis.shape, bf16),
            pltpu.VMEM((act_width, tokens), bf16),
            pltpu.VMEM((q_rows, act_width), bf16),
            pltpu.VMEM((seq_count, tiles, act_width, tile), bf16),
            pltpu.VMEM((tiles, act_width, tile), jnp.float32),
            pltpu.VMEM((seq_count, QUERIES, 8, 128), jnp.float32),
            dma((dp_count,)), dma((dp_count,)), dma((dp_count,)), dma((dp_count,)),
            dma((1, dp_count)), dma((1, dp_count)), dma((chunks, dp_count)), dma((chunks, dp_count)),
            dma((max(1, len(shared_train)), steps)), dma((max(1, len(shared_train)), steps)),
            dma((max(1, len(shared_query)), steps)), dma((max(1, len(shared_query)), steps)),
            dma((6,)), dma((tiles,)),
        ],
        compiler_params=pltpu.CompilerParams(
            collective_id=0, has_side_effects=True, vmem_limit_bytes=62 * 1024 * 1024),
    )(seq_lengths, act_in, grad_in, query_act, query_grad, act_basis, grad_basis)
    scale_seq = lax.rsqrt(seq_lengths.astype(jnp.float32))
    scores = partial[:, :seq_count] * scale_seq[None, :] / math.sqrt(QUERY_LEN * D * FF)
    return (moments, lax.psum(scores, ("dp", "mp")))


def solution(mesh):
    return jax.shard_map(
        local,
        mesh=mesh,
        in_specs=(
            P("dp", "mp"),
            P("dp", None),
            P("dp", "mp"),
            P("dp", None),
            P("mp", None),
            P("dp", None),
            P(),
        ),
        out_specs=(P("mp", "dp"), P()),
        check_vma=False,
    )
```

```python
import functools
import math

import jax
import jax.numpy as jnp
from jax import lax
from jax.experimental import pallas as pl
from jax.experimental.pallas import tpu as pltpu
from jax.sharding import PartitionSpec as P

D = 4096
FF = 16384
QUERIES = 64
QUERY_LEN = 16

damping = 0.1
MESH = pl.DeviceIdType.MESH


def flipped(index, mask):
    bit = 1
    while bit <= mask:
        if mask & bit:
            index = index + bit * (1 - 2 * ((index // bit) % 2))
        bit *= 2
    return index


def kernel(
    dp_count, mp_count, chunks, shared_train, shared_query,
    lengths, act_in, grad_in, query_act, query_grad, act_basis_in, grad_basis_in,
    moments, partial,
    act_raw, qact_raw, grad_raw, qgrad_raw, act_basis, grad_basis,
    act_t, q_rot, precond, staged, totals,
    act_send, act_recv, qact_send, qact_recv, grad_send, grad_recv, qgrad_send, qgrad_recv,
    pass_send, pass_recv, qpass_send, qpass_recv, local_sem, out_sem,
    shares, crossing, share_send, share_recv, cross_send, cross_recv,
):
    me = lax.axis_index("dp")
    mine = lax.axis_index("mp")
    seq_count = lengths.shape[0]
    tok_dev, act_width = act_in.shape
    q_dev = query_act.shape[0]
    cols = grad_raw.shape[2]
    block = act_basis_in.shape[1]
    tiles, _, tile = staged.shape
    tokens = tok_dev * dp_count
    seq_len = tokens // seq_count
    q_rows = q_dev * dp_count
    chunk_cols = cols // chunks
    masks = list(range(1, dp_count))
    peers = {k: flipped(me, k) for k in masks}

    barrier = pltpu.get_barrier_semaphore()
    for k in masks:
        pl.semaphore_signal(barrier, inc=1, device_id={"dp": peers[k], "mp": mine}, device_id_type=MESH)
    others = [lax.rem(mine + step, mp_count) for step in range(1, mp_count)]
    for other in others:
        pl.semaphore_signal(barrier, inc=1, device_id={"dp": me, "mp": other}, device_id_type=MESH)

    locals_in = [
        pltpu.make_async_copy(act_in, act_raw.at[me], local_sem.at[0]),
        pltpu.make_async_copy(act_basis_in, act_basis, local_sem.at[1]),
        pltpu.make_async_copy(grad_basis_in, grad_basis, local_sem.at[2]),
        pltpu.make_async_copy(
            grad_in.at[:, pl.ds(pl.multiple_of(me * cols, 128), cols)], grad_raw.at[me], local_sem.at[3]),
        pltpu.make_async_copy(query_act, qact_raw.at[me], local_sem.at[4]),
        pltpu.make_async_copy(
            query_grad.at[:, pl.ds(pl.multiple_of(me * cols, 128), cols)], qgrad_raw.at[me], local_sem.at[5]),
    ]
    for copy in locals_in:
        copy.start()
    pl.semaphore_wait(barrier, len(masks) + len(others))

    def remote(src, dst, send, recv, dp, mp):
        return pltpu.make_async_remote_copy(
            src_ref=src, dst_ref=dst, send_sem=send, recv_sem=recv,
            device_id={"dp": dp, "mp": mp}, device_id_type=MESH)

    sends = []

    def begin(copy):
        copy.start()
        sends.append(copy)

    act_masks = [k for k in masks if k == 1 or k % 2 == 0]

    def send_acts(src, raw, send, recv):
        for k in reversed(act_masks):
            begin(remote(src, raw.at[me], send.at[k], recv.at[k], peers[k], mine))

    def part_of(owner, rows):
        return pl.ds(pl.multiple_of(owner * (rows // mp_count), 16), rows // mp_count)

    def send_shared(src, raw, send, recv, shared):
        rows = part_of(mine, src.shape[0])
        for k in reversed(shared):
            there = pl.ds(pl.multiple_of(peers[k] * cols, 128), cols)
            begin(remote(
                src.at[rows, there], raw.at[me, rows, :], send.at[0, k], recv.at[0, k], peers[k], mine))

    def send_grads(src, raw, send, recv, shared, start, width, slot):
        for k in reversed(masks):
            if k not in shared:
                there = pl.ds(pl.multiple_of(peers[k] * cols + start, 128), width)
                begin(remote(
                    src.at[:, there], raw.at[me, :, pl.ds(start, width)],
                    send.at[slot, k], recv.at[slot, k], peers[k], mine))

    send_acts(act_in, act_raw, act_send, act_recv)
    send_shared(grad_in, grad_raw, grad_send, grad_recv, shared_train)
    send_shared(query_grad, qgrad_raw, qgrad_send, qgrad_recv, shared_query)
    send_grads(grad_in, grad_raw, grad_send, grad_recv, shared_train, 0, cols, 0)
    send_acts(query_act, qact_raw, qact_send, qact_recv)
    for c in range(chunks):
        send_grads(query_grad, qgrad_raw, qgrad_send, qgrad_recv, shared_query, c * chunk_cols, chunk_cols, c)

    def arrived(ref, send, recv):
        remote(ref, ref, send, recv, peers[1], mine).wait_recv()

    def relay_acts(raw, send, recv):
        for k in reversed(act_masks):
            arrived(raw.at[peers[k]], send.at[k], recv.at[k])
            if k > 1:
                here = raw.at[peers[k]]
                begin(remote(here, here, send.at[k + 1], recv.at[k + 1], peers[1], mine))

    def finish_acts(raw, send, recv):
        for k in masks:
            if k not in act_masks:
                arrived(raw.at[peers[k]], send.at[k], recv.at[k])

    def relay_grads(raw, send, recv, fsend, frecv, shared):
        for n, k in enumerate(reversed(shared)):
            here = raw.at[peers[k], part_of(mine, raw.shape[1]), :]
            arrived(here, send.at[0, k], recv.at[0, k])
            for step, other in enumerate(others):
                begin(remote(here, here, fsend.at[n, step], frecv.at[n, step], me, other))

    def finish_grads(raw, send, recv, shared, start, width, slot):
        for k in reversed(masks):
            if k not in shared:
                arrived(raw.at[peers[k], :, pl.ds(start, width)], send.at[slot, k], recv.at[slot, k])

    def finish_shared(raw, fsend, frecv, shared):
        for n, k in enumerate(reversed(shared)):
            for step in range(mp_count - 1):
                owner = lax.rem(mine + (mp_count - 1 - step), mp_count)
                arrived(
                    raw.at[peers[k], part_of(owner, raw.shape[1]), :], fsend.at[n, step], frecv.at[n, step])

    relay_acts(act_raw, act_send, act_recv)
    finish_acts(act_raw, act_send, act_recv)
    relay_grads(grad_raw, grad_send, grad_recv, pass_send, pass_recv, shared_train)
    relay_grads(qgrad_raw, qgrad_send, qgrad_recv, qpass_send, qpass_recv, shared_query)
    for copy in locals_in:
        copy.wait()

    limits = [lengths[s] for s in range(seq_count)]
    counted = limits[0]
    for s in range(1, seq_count):
        counted = counted + limits[s]
    inverse = 1.0 / jnp.full((1, tile), counted.astype(jnp.float32), jnp.float32)

    @pl.loop(0, dp_count)
    def _(e):
        where_tok = e * tok_dev + lax.broadcasted_iota(jnp.int32, (block, tok_dev), 1)
        live = jnp.zeros((block, tok_dev), jnp.float32)
        for s in range(seq_count):
            inside = (where_tok >= s * seq_len) & (where_tok < s * seq_len + limits[s])
            live = jnp.where(inside, 1.0, live)
        for b in range(act_width // block):
            span = pl.ds(b * block, block)
            turned = lax.dot_general(
                act_basis[span, :].T, act_raw[e, :, span], (((1,), (1,)), ((), ())),
                preferred_element_type=jnp.float32)
            act_t[span, pl.ds(pl.multiple_of(e * tok_dev, 128), tok_dev)] = (turned * live).astype(jnp.bfloat16)

    def wide_basis(jt):
        first = grad_basis[pl.ds(pl.multiple_of(jt * tile, 128), block), :]
        rows = []
        count = tile // block
        zero = jnp.zeros_like(first)
        for h in range(count):
            own = grad_basis[pl.ds(pl.multiple_of(jt * tile + h * block, 128), block), :]
            rows.append(jnp.concatenate([own if g == h else zero for g in range(count)], axis=1))
        return jnp.concatenate(rows, axis=0)

    def turned_grads(raw, jt, rows):
        span = pl.ds(pl.multiple_of(jt * tile, 128), tile)
        whole = raw[:, :, span].reshape(rows, tile)
        return jnp.dot(whole, wide_basis(jt), preferred_element_type=jnp.float32).astype(jnp.bfloat16)

    finish_shared(grad_raw, pass_send, pass_recv, shared_train)
    finish_grads(grad_raw, grad_send, grad_recv, shared_train, 0, cols, 0)

    def out_copy(jt):
        span = pl.ds(pl.multiple_of(jt * tile, 128), tile)
        return pltpu.make_async_copy(staged.at[jt], moments.at[:, span], out_sem.at[jt])

    per_chunk = tiles // chunks

    def first_phase(jt):
        grads = turned_grads(grad_raw, jt, tokens)
        total = jnp.zeros((act_width, tile), jnp.float32)
        for s in range(seq_count):
            a = act_t[:, s * seq_len:(s + 1) * seq_len]
            g = grads[s * seq_len:(s + 1) * seq_len, :]
            total = total + jnp.dot(a * a, g * g, preferred_element_type=jnp.float32)
        total = total * inverse
        staged[jt] = total
        weights = 1.0 / (total + damping)
        for s in range(seq_count):
            a = act_t[:, s * seq_len:(s + 1) * seq_len]
            g = grads[s * seq_len:(s + 1) * seq_len, :]
            precond[s, jt] = (weights * jnp.dot(a, g, preferred_element_type=jnp.float32)).astype(jnp.bfloat16)
        out_copy(jt).start()

    half = tiles // 2
    pl.loop(0, half)(first_phase)
    relay_acts(qact_raw, qact_send, qact_recv)
    pl.loop(half, tiles)(first_phase)
    finish_acts(qact_raw, qact_send, qact_recv)

    @pl.loop(0, dp_count)
    def _(e):
        for b in range(act_width // block):
            span = pl.ds(b * block, block)
            turned = jnp.dot(qact_raw[e, :, span], act_basis[span, :], preferred_element_type=jnp.float32)
            q_rot[pl.ds(pl.multiple_of(e * q_dev, 16), q_dev), span] = turned.astype(jnp.bfloat16)

    totals[...] = jnp.zeros_like(totals)
    finish_shared(qgrad_raw, qpass_send, qpass_recv, shared_query)

    def second_phase(jt):
        grads = turned_grads(qgrad_raw, jt, q_rows).astype(jnp.float32)
        for s in range(seq_count):
            mapped = jnp.dot(q_rot[...], precond[s, jt], preferred_element_type=jnp.float32) * grads
            folded = mapped[:, :128]
            for h in range(1, tile // 128):
                folded = folded + mapped[:, h * 128:(h + 1) * 128]
            totals[s] += folded.reshape(QUERIES, q_rows // QUERIES // 8, 8, 128).sum(axis=1)

    for c in range(chunks):
        finish_grads(qgrad_raw, qgrad_send, qgrad_recv, shared_query, c * chunk_cols, chunk_cols, c)
        pl.loop(c * per_chunk, (c + 1) * per_chunk)(second_phase)

    lane = lax.broadcasted_iota(jnp.int32, (QUERIES, 128), 1)
    answer = jnp.zeros((QUERIES, 128), jnp.float32)
    for s in range(seq_count):
        row = jnp.sum(jnp.sum(totals[s], axis=1), axis=1, keepdims=True)
        answer = jnp.where(lane == s, row, answer)
    lens = jnp.ones((QUERIES, 128), jnp.float32)
    for s in range(seq_count):
        lens = jnp.where(lane == s, limits[s].astype(jnp.float32), lens)
    shares[me] = answer * lax.rsqrt(lens) / math.sqrt(QUERY_LEN * D * FF)

    for jt in range(tiles):
        out_copy(jt).wait()
    for copy in sends:
        copy.wait_send()
    sends.clear()

    for k in masks:
        begin(remote(shares.at[me], shares.at[me], share_send.at[k], share_recv.at[k], peers[k], mine))
    for k in masks:
        arrived(shares.at[peers[k]], share_send.at[k], share_recv.at[k])
    summed = shares[0]
    for e in range(1, dp_count):
        summed = summed + shares[e]
    crossing[mine] = summed
    for step, other in enumerate(others):
        begin(remote(
            crossing.at[mine], crossing.at[mine], cross_send.at[step], cross_recv.at[step], me, other))
    for step in range(mp_count - 1):
        owner = lax.rem(mine + (mp_count - 1 - step), mp_count)
        arrived(crossing.at[owner], cross_send.at[step], cross_recv.at[step])
    summed = crossing[0]
    for e in range(1, mp_count):
        summed = summed + crossing[e]
    partial[...] = summed[:, :seq_count]
    for copy in sends:
        copy.wait_send()


def local(act_in, grad_in, query_act, query_grad, act_basis, grad_basis, seq_lengths):
    dp_count = lax.axis_size("dp")
    mp_count = lax.axis_size("mp")
    tok_dev, act_width = act_in.shape
    q_dev = query_act.shape[0]
    cols = grad_in.shape[1] // dp_count
    seq_count = seq_lengths.shape[0]
    tokens, q_rows = tok_dev * dp_count, q_dev * dp_count
    tile = min(256, cols)
    tiles = cols // tile
    chunks = min(4, tiles)
    far = [k for k in range(1, dp_count) if bin(k >> 1).count("1") >= 2]
    shared_train = far if tok_dev % (16 * mp_count) == 0 and dp_count <= 2 * tiles else []
    shared_query = far if q_dev % (16 * mp_count) == 0 and dp_count <= 2 * tiles else []
    steps = max(1, mp_count - 1)
    dma = pltpu.SemaphoreType.DMA
    any_space = pl.BlockSpec(memory_space=pl.ANY)
    bf16 = jnp.bfloat16
    return pl.pallas_call(
        functools.partial(kernel, dp_count, mp_count, chunks, shared_train, shared_query),
        out_shape=(
            jax.ShapeDtypeStruct((act_width, cols), jnp.float32),
            jax.ShapeDtypeStruct((QUERIES, seq_count), jnp.float32),
        ),
        in_specs=[pl.BlockSpec(memory_space=pltpu.SMEM)] + [any_space] * 6,
        out_specs=(any_space, pl.BlockSpec(memory_space=pltpu.VMEM)),
        scratch_shapes=[
            pltpu.VMEM((dp_count, tok_dev, act_width), bf16),
            pltpu.VMEM((dp_count, q_dev, act_width), bf16),
            pltpu.VMEM((dp_count, tok_dev, cols), bf16),
            pltpu.VMEM((dp_count, q_dev, cols), bf16),
            pltpu.VMEM(act_basis.shape, bf16),
            pltpu.VMEM(grad_basis.shape, bf16),
            pltpu.VMEM((act_width, tokens), bf16),
            pltpu.VMEM((q_rows, act_width), bf16),
            pltpu.VMEM((seq_count, tiles, act_width, tile), bf16),
            pltpu.VMEM((tiles, act_width, tile), jnp.float32),
            pltpu.VMEM((seq_count, QUERIES, 8, 128), jnp.float32),
            dma((dp_count,)), dma((dp_count,)), dma((dp_count,)), dma((dp_count,)),
            dma((1, dp_count)), dma((1, dp_count)), dma((chunks, dp_count)), dma((chunks, dp_count)),
            dma((max(1, len(shared_train)), steps)), dma((max(1, len(shared_train)), steps)),
            dma((max(1, len(shared_query)), steps)), dma((max(1, len(shared_query)), steps)),
            dma((6,)), dma((tiles,)),
            pltpu.VMEM((dp_count, QUERIES, 128), jnp.float32),
            pltpu.VMEM((mp_count, QUERIES, 128), jnp.float32),
            dma((dp_count,)), dma((dp_count,)), dma((steps,)), dma((steps,)),
        ],
        compiler_params=pltpu.CompilerParams(
            collective_id=0, has_side_effects=True, vmem_limit_bytes=62 * 1024 * 1024),
    )(seq_lengths, act_in, grad_in, query_act, query_grad, act_basis, grad_basis)


def solution(mesh):
    return jax.shard_map(
        local,
        mesh=mesh,
        in_specs=(
            P("dp", "mp"),
            P("dp", None),
            P("dp", "mp"),
            P("dp", None),
            P("mp", None),
            P("dp", None),
            P(),
        ),
        out_specs=(P("mp", "dp"), P()),
        check_vma=False,
    )
```
